512 devices in a mesh: dp: 16 (over z), tensor: 32 (over x, y, core).
Axes of the slice: x: 4, y: 4, z: 16, core: 2. Of those that a mesh axis runs over, the one named last changes fastest.
Arguments:
- hidden: bfloat16 [14336, 4096], P('dp', 'tensor')
- gain: bfloat16 [4096], P('tensor'), may hold values from 0.5 to 1.5
- head_weight: bfloat16 [4096, 32000], P('dp', 'tensor')
- targets: int32 [14336], P('dp'), may hold values from 0 to 31999
- seq_ids: int32 [14336], P(('dp', 'tensor')), may hold values from 0 to 63, never falling along the last dimension, each value on 1 to 1792 neighbouring positions
- live: int32 [14336], P(('dp', 'tensor')), may hold values 0 or 1
Outputs:
- logprob: float32 [14336], P(('dp', 'tensor'))
- entropy: float32 [14336], P(('dp', 'tensor'))
- seq_mean: float32 [64], replicated
The draws below stay inside these ranges and needn't reach their ends.
Inputs may be any that keep to these rules, and one draw needn't show every extreme that they name: `seq_ids`: sequence numbers never fall along the tokens; each sequence has 1 to 1792 tokens, one exactly 1792.
All inputs are finite; a program needn't handle non-finite values. No bound on the sum of `live` on one device may be relied on, other than what follows from the above.
Results may differ from the reference program's by a relative error of at most 0.0015.
Values may be sent and summed in bfloat16 or wider, within the bound.
No kernel may reach another device: no remote copies, remote signals or barrier semaphores. Data moves between devices by JAX's collectives and lax.ppermute only.
A program may use at most 64 MiB of HBM per device.

```python
import math
import jax
import jax.numpy as jnp
import numpy as np
from jax import lax

D = 4096
V = 32000
TOKENS = 14336
SEQS = 64
LONGEST = 1792


def column_of(key, index):
    return jax.random.normal(jax.random.fold_in(key, index), (D,), jnp.float32) * 3.0 / math.sqrt(D)


def column_table(key, indices):

    def single(index):
        return column_of(key, index)
    return jax.vmap(single)(indices)


def draw_head_weight(key, part):
    weight_key = jax.random.fold_in(key, 13)
    full = column_table(weight_key, jnp.arange(V)).T
    return full.astype(jnp.bfloat16)


def draw_hidden(key, part):
    row_key = jax.random.fold_in(key, 14)
    row_scale = jnp.exp(jax.random.uniform(jax.random.fold_in(key, 15), (TOKENS, 1), jnp.float32, 0.0, math.log(10.0)))
    col_scale = jnp.exp(jax.random.uniform(jax.random.fold_in(key, 16), (1, D), jnp.float32, 0.0, math.log(10.0)))
    base = jax.random.normal(row_key, (TOKENS, D), jnp.float32)
    values = base * row_scale * col_scale
    return values.astype(jnp.bfloat16)


def plant(entries, rng, low, top_value):
    longest = entries.shape.index(max(entries.shape))
    spots = []
    for shift in (0, 1):
        where = [jax.random.randint(jax.random.fold_in(rng, axis), (), 0, length) for axis, length in enumerate(entries.shape)]
        where[longest] = (where[longest] + shift) % entries.shape[longest]
        spots.append(tuple(where))
    return entries.at[spots[0]].set(low).at[spots[1]].set(top_value)


def rank_table(number_of, slope):
    loads = [(1 << 20) // math.isqrt(grade ** slope) + 1 for grade in range(1, number_of + 1)]
    scale = 1 + sum(loads) // (1 << 30)
    return np.cumsum(np.array([max(1, weight // scale) for weight in loads]))


def ranked(key, dims, number_of, lean):
    listing = rank_table(number_of, lean)
    pick = jax.random.randint(jax.random.fold_in(key, 1), dims, 0, int(listing[number_of - 1]))
    grade = jnp.searchsorted(jnp.asarray(listing, jnp.int32), pick, side="right")
    return jax.random.permutation(jax.random.fold_in(key, 2), number_of)[grade].astype(jnp.int32)


def profile(amount, total, bound, slope):
    loads = [(1 << 20) // math.isqrt(standing ** slope) + 1 for standing in range(2, amount + 1)]
    surplus, given = total - bound - (amount - 1), [1] * (amount - 1)
    while surplus > 0:
        free = [i for i in range(amount - 1) if given[i] < bound]
        mass, left = sum([loads[i] for i in free]), surplus
        for i in free:
            addition = min(bound - given[i], max(1, left * loads[i] // mass), surplus)
            given[i] = given[i] + addition
            surplus = surplus - addition
    return np.array([bound] + given)


def ragged_sizes(stream_key, amount, total, bound, skew):
    if amount == 2:
        one = jax.random.randint(stream_key, (), max(1, total - bound), min(bound, total - 1) + 1)
        return jnp.stack([one, total - one])
    sizes = jnp.asarray(profile(amount, total, bound, skew), jnp.int32)
    pairs = (amount - 1) // 2
    giver, receiver = sizes[1:1 + 2 * pairs:2], sizes[2:2 + 2 * pairs:2]
    slack = jnp.minimum(giver - 1, bound - receiver)
    moved = jax.random.randint(jax.random.fold_in(stream_key, 1), (pairs,), 0, 1 << 20) % (slack + 1)
    sizes = sizes.at[1:1 + 2 * pairs:2].set(giver - moved).at[2:2 + 2 * pairs:2].set(receiver + moved)
    return sizes[jax.random.permutation(jax.random.fold_in(stream_key, 2), amount)]


def setup_inputs(seed: int = 0) -> dict:
    keys = jax.random.split(jax.random.key(seed), 7)
    hidden = draw_hidden(jax.random.fold_in(keys[6], 71), 0)
    gain = jnp.clip(1.0 + 0.1 * jax.random.normal(keys[1], (D,), jnp.float32), 0.5, 1.5).astype(jnp.bfloat16)
    head_weight = draw_head_weight(jax.random.fold_in(keys[6], 71), 0)
    targets = plant(ranked(keys[3], (TOKENS,), V, 2), jax.random.fold_in(keys[3], 3), 0, V - 1).astype(jnp.int32)
    seq_ids = jnp.searchsorted(jnp.cumsum(ragged_sizes(keys[4], SEQS, TOKENS, LONGEST, 2)), jnp.arange(TOKENS), side="right").astype(jnp.int32)
    live = plant((jax.random.randint(keys[5], (TOKENS,), 0, 8) < 7).astype(jnp.int32), jax.random.fold_in(keys[5], 1), 0, 1)
    return dict(hidden=hidden, gain=gain, head_weight=head_weight, targets=targets, seq_ids=seq_ids, live=live)


def reference(hidden, gain, head_weight, targets, seq_ids, live):
    values = hidden.astype(jnp.float32)
    meansq = lax.optimization_barrier(jnp.mean(values * values, axis=-1, keepdims=True))
    normed = (values * lax.rsqrt(meansq + 1e-05) * gain.astype(jnp.float32)).astype(jnp.bfloat16)
    width = min(512, TOKENS)
    blocks = normed.reshape(TOKENS // width, width, D)
    chosen = targets.reshape(TOKENS // width, width)

    def one_block(pair):
        rows, picks = pair
        scores = jnp.dot(rows, head_weight, preferred_element_type=jnp.float32)
        top = lax.optimization_barrier(jnp.max(scores, axis=-1, keepdims=True))
        shifted = scores - top
        expo = jnp.exp(shifted)
        total = lax.optimization_barrier(jnp.sum(expo, axis=-1))
        spread = lax.optimization_barrier(jnp.sum(expo * shifted, axis=-1))
        target_score = jnp.take_along_axis(scores, picks[:, None], axis=1)[:, 0]
        logp = target_score - top[:, 0] - jnp.log(total)
        entro = jnp.log(total) - spread / total
        return (logp, entro)
    logp, entro = lax.map(one_block, (blocks, chosen))
    weight = live.astype(jnp.float32)
    logprob = logp.reshape(TOKENS) * weight
    entropy = entro.reshape(TOKENS) * weight
    sums = jax.ops.segment_sum(logprob, seq_ids, num_segments=SEQS)
    counts = jax.ops.segment_sum(weight, seq_ids, num_segments=SEQS)
    seq_mean = sums / jnp.maximum(counts, 1.0)
    return (logprob, entropy, seq_mean)
```

```python
import functools

import jax
import jax.numpy as jnp
from jax import lax
from jax.experimental import pallas as pl
from jax.experimental.pallas import tpu as pltpu
from jax.sharding import PartitionSpec as P


SEQS = 64
EXTRA = 16
VM = pl.BlockSpec(memory_space=pltpu.VMEM)
SM = pl.BlockSpec(memory_space=pltpu.SMEM)
NT = (((1,), (1,)), ((), ()))


def room(mib):
    return pltpu.CompilerParams(vmem_limit_bytes=mib << 20)


def cost(flops, nbytes):
    return pl.CostEstimate(flops=int(flops), transcendentals=0, bytes_accessed=int(nbytes))


def fan_kernel(hid_ref, gain_ref, seq_ref, live_ref, out_ref, block_ref, extra_ref, sems):
    copies, rows, _ = out_ref.shape
    share = seq_ref.shape[1]
    extra_ref[...] = jnp.zeros_like(extra_ref)
    extra_ref[0:1, :] = gain_ref[...].astype(jnp.float32)
    extra_ref[1:2, 0:share] = seq_ref[...].astype(jnp.float32)
    extra_ref[2:3, 0:share] = live_ref[...].astype(jnp.float32)
    block_ref[0 : rows - EXTRA, :] = hid_ref[...]
    block_ref[rows - EXTRA : rows, :] = extra_ref[...].astype(jnp.bfloat16)
    moves = [pltpu.make_async_copy(block_ref, out_ref.at[i], sems.at[i]) for i in range(copies)]
    for move in moves:
        move.start()
    for move in moves:
        move.wait()


def fan(hidden, gain, seq_ids, live, copies):
    tokens, lanes = hidden.shape
    return pl.pallas_call(
        fan_kernel,
        out_shape=jax.ShapeDtypeStruct((copies, tokens + EXTRA, lanes), jnp.bfloat16),
        in_specs=[VM] * 4,
        out_specs=pl.BlockSpec(memory_space=pltpu.HBM),
        scratch_shapes=[
            pltpu.VMEM((tokens + EXTRA, lanes), jnp.bfloat16),
            pltpu.VMEM((EXTRA, lanes), jnp.float32),
            pltpu.SemaphoreType.DMA((copies,)),
        ],
        compiler_params=room(4),
        name="fan",
    )(hidden, gain[None], seq_ids[None], live[None])


def norm_kernel(core_ref, one_ref, two_ref, out_ref):
    chips, rows, lanes = one_ref.shape
    tokens = rows - EXTRA
    step = 128
    core = core_ref[0]

    def block(i, carry):
        at = pl.ds(pl.multiple_of(i * step, step), step)
        square = jnp.zeros((step, lanes), jnp.float32)
        for ref in (one_ref, two_ref):
            for t in range(chips):
                v = ref[t, at, :].astype(jnp.float32)
                square = square + v * v
        mean = jnp.sum(square, axis=-1, keepdims=True) / (2 * chips * lanes)
        scale = lax.rsqrt(mean + 1e-05)
        for ref, half in ((one_ref, core), (two_ref, 1 - core)):
            to = pl.ds(pl.multiple_of(half * lanes, lanes), lanes)
            for t in range(chips):
                v = ref[t, at, :].astype(jnp.float32)
                gain = ref[t, tokens:rows, :].astype(jnp.float32)[0:1, :]
                out_ref[t, at, to] = (v * scale * gain).astype(jnp.bfloat16)
        return carry

    lax.fori_loop(0, tokens // step, block, 0)


def normalise(core, one, two):
    chips, rows, lanes = one.shape
    tokens = rows - EXTRA
    return pl.pallas_call(
        norm_kernel,
        out_shape=jax.ShapeDtypeStruct((chips, tokens, 2 * lanes), jnp.bfloat16),
        in_specs=[SM, VM, VM],
        out_specs=VM,
        compiler_params=room(20),
        cost_estimate=cost(12 * one.size, 8 * one.size),
        name="norm",
    )(core, one, two)


def product(w, x):
    return lax.dot_general(w, x, NT, preferred_element_type=jnp.float32)


def blocks_of(tokens, width=256):
    return [slice(i, min(i + width, tokens)) for i in range(0, tokens, width)]


def mm_kernel(count, fresh, at_ref, n_ref, *refs):
    ws, out_ref = refs[:count], refs[-1]
    for cols in blocks_of(n_ref.shape[1]):
        total = None if fresh else refs[count][:, cols]
        for i in range(count):
            d = product(ws[i][...], n_ref[at_ref[i], cols, :])
            total = d if total is None else total + d
        out_ref[:, cols] = total


def accumulate(at, normed, ws, acc=None):
    vocab, depth = ws[0].shape
    tokens = normed.shape[1]
    return pl.pallas_call(
        functools.partial(mm_kernel, len(ws), acc is None),
        out_shape=jax.ShapeDtypeStruct((vocab, tokens), jnp.float32),
        in_specs=[SM, VM] + [VM] * len(ws) + ([] if acc is None else [VM]),
        out_specs=VM,
        input_output_aliases={} if acc is None else {2 + len(ws): 0},
        compiler_params=room(26),
        cost_estimate=cost(2 * len(ws) * vocab * depth * tokens, 8 * vocab * tokens),
        name="scores",
    )(at, normed, *ws, *([] if acc is None else [acc]))


def stats_kernel(at_ref, n_ref, w_ref, acc_ref, ids_ref, out_ref, s_ref):
    _, tokens = acc_ref.shape
    for cols in blocks_of(tokens):
        s_ref[:, cols] = acc_ref[:, cols] + product(w_ref[...], n_ref[at_ref[0], cols, :])
    for j in range(tokens // 128):
        at = slice(j * 128, (j + 1) * 128)
        s = s_ref[:, at]
        top = jnp.max(s, axis=0, keepdims=True)
        row = lax.broadcasted_iota(jnp.int32, s.shape, 0)
        picked = jnp.sum(jnp.where(row == ids_ref[:, at], s, 0.0), axis=0, keepdims=True)
        shifted = s - top
        expo = jnp.exp(shifted)
        total = jnp.sum(expo, axis=0, keepdims=True)
        spread = jnp.sum(expo * shifted, axis=0, keepdims=True)
        out_ref[0:1, at] = top
        out_ref[1:2, at] = total
        out_ref[2:3, at] = spread
        out_ref[3:4, at] = picked


def statistics(at, normed, w, acc, ids):
    vocab, tokens = acc.shape
    return pl.pallas_call(
        stats_kernel,
        out_shape=jax.ShapeDtypeStruct((4, tokens), jnp.float32),
        in_specs=[SM, VM, VM, VM, VM],
        out_specs=VM,
        scratch_shapes=[pltpu.VMEM((vocab, tokens), jnp.float32)],
        compiler_params=room(26),
        cost_estimate=cost(2 * vocab * w.shape[1] * tokens, 8 * vocab * tokens),
        name="stats",
    )(at, normed, w, acc, ids)


def combine_kernel(x_ref, seq_ref, live_ref, logprob_ref, entropy_ref, sums_ref):
    top = x_ref[:, 0, :]
    total = x_ref[:, 1, :]
    best = jnp.max(top, axis=0, keepdims=True)
    gap = top - best
    scale = jnp.exp(gap)
    g_total = jnp.sum(total * scale, axis=0, keepdims=True)
    g_spread = jnp.sum((x_ref[:, 2, :] + gap * total) * scale, axis=0, keepdims=True)
    g_target = jnp.sum(x_ref[:, 3, :], axis=0, keepdims=True)
    live = live_ref[...]
    log_total = jnp.log(g_total)
    logprob = (g_target - best - log_total) * live
    logprob_ref[...] = logprob
    entropy_ref[...] = (log_total - g_spread / g_total) * live
    tokens = top.shape[1]
    row = lax.broadcasted_iota(jnp.int32, (8, tokens), 0)
    both = jnp.where(row == 0, logprob, jnp.where(row == 1, live, 0.0))
    seat = lax.broadcasted_iota(jnp.int32, (2 * SEQS, tokens), 0) % SEQS
    member = (seat == seq_ref[...]).astype(jnp.float32)
    sums = lax.dot_general(
        both, member, NT, precision=lax.Precision.HIGHEST, preferred_element_type=jnp.float32
    )
    lane = lax.broadcasted_iota(jnp.int32, (1, 2 * SEQS), 1)
    sums_ref[...] = jnp.where(lane < SEQS, sums[0:1, :], sums[1:2, :])


def combine(x, seq, live):
    tokens = x.shape[2]
    row = jax.ShapeDtypeStruct((1, tokens), jnp.float32)
    return pl.pallas_call(
        combine_kernel,
        out_shape=(row, row, jax.ShapeDtypeStruct((1, 2 * SEQS), jnp.float32)),
        in_specs=[VM] * 3,
        out_specs=(VM, VM, VM),
        compiler_params=room(8),
        name="combine",
    )(x, seq, live)


def body(hidden, gain, head_weight, targets, seq_ids, live):
    shards = lax.axis_size("tensor")
    ring = lax.axis_size("dp")
    rank, z = lax.axis_index("tensor"), lax.axis_index("dp")
    tokens = hidden.shape[0]
    share = tokens // shards
    vocab_dev = head_weight.shape[1]

    forth = [(i, (i + 1) % ring) for i in range(ring)]
    back = [(i, (i - 1) % ring) for i in range(ring)]
    own = head_weight.T
    chunks = [own]

    def turn(a, b, s):
        a = lax.ppermute(a, "dp", forth)
        if s < ring - s:
            b = lax.ppermute(b, "dp", back)
            return a, b
        return a, None

    tie = lax.optimization_barrier
    a, b = turn(own, own, 1)
    core = rank % 2
    teams = [[t for t in range(shards) if t % 2 == c] for c in range(2)]
    sent = fan(hidden, gain, seq_ids, live, shards // 2)
    one = lax.all_to_all(sent, "tensor", 0, 0, axis_index_groups=teams)
    chunks += [a, b]
    for s in range(2, 5):
        a, b = turn(a, b, s)
        if s == 4:
            a, b, one = tie((a, b, one))
        chunks += [a, b]
    two = lax.ppermute(one, "tensor", [(t, t ^ 1) for t in range(shards)])
    a, b = turn(a, b, 5)
    chunks += [a, b]
    normed = normalise(core[None].astype(jnp.int32), one, two)

    def pick(lo, hi):
        span = [z] + [z + (s if i else -s) for s in range(1, ring // 2 + 1) for i in range(2)]
        return (jnp.stack(span[lo:hi]) % ring).astype(jnp.int32)

    a, b = turn(a, b, 6)
    a, b, normed = tie((a, b, normed))
    chunks += [a, b]
    acc = accumulate(pick(0, 9), normed, chunks[0:9])
    a, b = turn(a, b, 7)
    a, b, acc = tie((a, b, acc))
    chunks += [a, b]
    acc = accumulate(pick(9, 15), normed, chunks[9:15], acc)
    a, _ = turn(a, b, 8)
    flags = jnp.stack([one, two])[:, :, tokens + 1 : tokens + 3, :share].astype(jnp.float32)
    flags = jnp.where(core == 0, flags, flags[::-1]).transpose(2, 1, 0, 3).reshape(2, 1, tokens)
    seq, alive = flags[0].astype(jnp.int32), flags[1]
    stats = statistics(pick(15, 16), normed, a, acc, (targets - rank * vocab_dev)[None])

    everyone = lax.all_to_all(
        jnp.broadcast_to(stats[None], (shards, *stats.shape)), "tensor", 0, 0
    )
    logprob, entropy, sums = combine(everyone, seq, alive)
    planes = lax.all_to_all(jnp.broadcast_to(sums, (ring, 2 * SEQS)), "dp", 0, 0)
    whole = jnp.sum(planes, axis=0)
    seq_mean = whole[:SEQS] / jnp.maximum(whole[SEQS:], 1.0)
    mine = functools.partial(lax.dynamic_slice_in_dim, start_index=rank * share, slice_size=share)
    return mine(logprob[0]), mine(entropy[0]), seq_mean


def solution(mesh):
    placed = (
        P("dp", "tensor"),
        P("tensor"),
        P("dp", "tensor"),
        P("dp"),
        P(("dp", "tensor")),
        P(("dp", "tensor")),
    )

    return jax.shard_map(
        body,
        mesh=mesh,
        in_specs=placed,
        out_specs=(P(("dp", "tensor")), P(("dp", "tensor")), P()),
        check_vma=False,
    )
```

```python
import functools

import jax
import jax.numpy as jnp
from jax import lax
from jax.experimental import pallas as pl
from jax.experimental.pallas import tpu as pltpu
from jax.sharding import PartitionSpec as P


SEQS = 64
EXTRA = 16
VM = pl.BlockSpec(memory_space=pltpu.VMEM)
NT = (((1,), (1,)), ((), ()))


def room(mib):
    return pltpu.CompilerParams(vmem_limit_bytes=mib << 20)


def cost(flops, nbytes):
    return pl.CostEstimate(flops=int(flops), transcendentals=0, bytes_accessed=int(nbytes))


def fan_kernel(hid_ref, gain_ref, seq_ref, live_ref, out_ref, block_ref, g_ref, s_ref, l_ref, extra_ref, sems):
    copies, rows, _ = out_ref.shape
    share = seq_ref.shape[1]
    loads = [
        pltpu.make_async_copy(gain_ref, g_ref, sems.at[0]),
        pltpu.make_async_copy(seq_ref, s_ref, sems.at[1]),
        pltpu.make_async_copy(live_ref, l_ref, sems.at[2]),
        pltpu.make_async_copy(hid_ref, block_ref.at[pl.ds(0, rows - EXTRA)], sems.at[3]),
    ]
    for load in loads:
        load.start()
    for load in loads:
        load.wait()
    extra_ref[...] = jnp.zeros_like(extra_ref)
    extra_ref[0:1, :] = g_ref[...].astype(jnp.float32)
    extra_ref[1:2, 0:share] = s_ref[...].astype(jnp.float32)
    extra_ref[2:3, 0:share] = l_ref[...].astype(jnp.float32)
    block_ref[rows - EXTRA : rows, :] = extra_ref[...].astype(jnp.bfloat16)
    moves = [pltpu.make_async_copy(block_ref, out_ref.at[i], sems.at[i]) for i in range(copies)]
    for move in moves:
        move.start()
    for move in moves:
        move.wait()


def fan(hidden, gain, seq_ids, live, copies):
    tokens, lanes = hidden.shape
    share = seq_ids.shape[0]
    return pl.pallas_call(
        fan_kernel,
        out_shape=pltpu.HBM((copies, tokens + EXTRA, lanes), jnp.bfloat16),
        in_specs=[pl.BlockSpec(memory_space=pltpu.HBM)] * 4,
        out_specs=pl.BlockSpec(memory_space=pltpu.HBM),
        scratch_shapes=[
            pltpu.VMEM((tokens + EXTRA, lanes), jnp.bfloat16),
            pltpu.VMEM((1, lanes), jnp.bfloat16),
            pltpu.VMEM((1, share), jnp.int32),
            pltpu.VMEM((1, share), jnp.int32),
            pltpu.VMEM((EXTRA, lanes), jnp.float32),
            pltpu.SemaphoreType.DMA((copies,)),
        ],
        compiler_params=room(4),
        name="fan",
    )(hidden, gain[None], seq_ids[None], live[None])


def norm_kernel(one_ref, two_ref, gain_one_ref, gain_two_ref, out_ref, flag_ref):
    chips, step, lanes = one_ref.shape
    core = lax.axis_index("tensor") % 2

    @pl.when(pl.program_id(0) == 0)
    def _():
        flag_ref[core] = gain_one_ref[...].astype(jnp.float32)
        flag_ref[1 - core] = gain_two_ref[...].astype(jnp.float32)

    square = jnp.zeros((step, lanes), jnp.float32)
    for ref in (one_ref, two_ref):
        for t in range(chips):
            v = ref[t].astype(jnp.float32)
            square = square + v * v
    mean = jnp.sum(square, axis=-1, keepdims=True) / (2 * chips * lanes)
    scale = lax.rsqrt(mean + 1e-05)
    for ref, gain_ref, half in ((one_ref, gain_one_ref, core), (two_ref, gain_two_ref, 1 - core)):
        to = pl.ds(pl.multiple_of(half * lanes, lanes), lanes)
        for t in range(chips):
            gain = gain_ref[t].astype(jnp.float32)[0:1, :]
            out_ref[t, :, to] = (ref[t].astype(jnp.float32) * scale * gain).astype(jnp.bfloat16)


def normalise(one, two):
    chips, rows, lanes = one.shape
    tokens, step = rows - EXTRA, 128
    part = pl.BlockSpec((chips, step, lanes), lambda i: (0, i, 0))
    gain = pl.BlockSpec((chips, EXTRA, lanes), lambda i: (0, tokens // EXTRA, 0))
    return pl.pallas_call(
        norm_kernel,
        grid=(tokens // step,),
        out_shape=(
            jax.ShapeDtypeStruct((chips, tokens, 2 * lanes), jnp.bfloat16),
            jax.ShapeDtypeStruct((2, chips, EXTRA, lanes), jnp.float32),
        ),
        in_specs=[part, part, gain, gain],
        out_specs=(
            pl.BlockSpec((chips, step, 2 * lanes), lambda i: (0, i, 0)),
            pl.BlockSpec((2, chips, EXTRA, lanes), lambda i: (0, 0, 0, 0)),
        ),
        compiler_params=room(8),
        cost_estimate=cost(12 * one.size, 8 * one.size),
        name="norm",
    )(one, two, one, two)


def product(w, x):
    return lax.dot_general(w, x, NT, preferred_element_type=jnp.float32)


def blocks_of(tokens, width=256):
    return [slice(i, min(i + width, tokens)) for i in range(0, tokens, width)]


def row_block(ahead):
    return (lax.axis_index("dp") + ahead) % lax.axis_size("dp")


def mm_kernel(aheads, n_ref, *refs):
    count = len(aheads)
    ws, out_ref = refs[:count], refs[-1]
    fresh = len(refs) == count + 1
    at = [row_block(ahead + n_ref.shape[0]) for ahead in aheads]
    for cols in blocks_of(n_ref.shape[1]):
        total = None if fresh else refs[count][:, cols]
        for i in range(count):
            d = product(ws[i][...], n_ref[at[i], cols, :])
            total = d if total is None else total + d
        out_ref[:, cols] = total


def accumulate(aheads, normed, ws, acc=None):
    vocab, depth = ws[0].shape
    tokens = normed.shape[1]
    return pl.pallas_call(
        functools.partial(mm_kernel, tuple(aheads)),
        out_shape=jax.ShapeDtypeStruct((vocab, tokens), jnp.float32),
        in_specs=[VM] * (1 + len(ws)) + ([] if acc is None else [VM]),
        out_specs=VM,
        input_output_aliases={} if acc is None else {1 + len(ws): 0},
        compiler_params=room(12),
        cost_estimate=cost(2 * len(ws) * vocab * depth * tokens, 8 * vocab * tokens),
        name="scores",
    )(normed, *ws, *([] if acc is None else [acc]))


def stats_kernel(ahead, n_ref, w_ref, acc_ref, ids_ref, out_ref, s_ref):
    vocab, tokens = acc_ref.shape
    at = row_block(ahead)
    first = lax.axis_index("tensor") * vocab
    for cols in blocks_of(tokens):
        s_ref[:, cols] = acc_ref[:, cols] + product(w_ref[...], n_ref[at, cols, :])
    for j in range(tokens // 128):
        at = slice(j * 128, (j + 1) * 128)
        s = s_ref[:, at]
        top = jnp.max(s, axis=0, keepdims=True)
        row = lax.broadcasted_iota(jnp.int32, s.shape, 0)
        picked = jnp.sum(jnp.where(row == ids_ref[at][None] - first, s, 0.0), axis=0, keepdims=True)
        shifted = s - top
        expo = jnp.exp(shifted)
        total = jnp.sum(expo, axis=0, keepdims=True)
        spread = jnp.sum(expo * shifted, axis=0, keepdims=True)
        out_ref[0:1, at] = top
        out_ref[1:2, at] = total
        out_ref[2:3, at] = spread
        out_ref[3:4, at] = picked


def statistics(ahead, normed, w, acc, ids):
    vocab, tokens = acc.shape
    return pl.pallas_call(
        functools.partial(stats_kernel, ahead),
        out_shape=jax.ShapeDtypeStruct((4, tokens), jnp.float32),
        in_specs=[VM] * 4,
        out_specs=VM,
        scratch_shapes=[pltpu.VMEM((vocab, tokens), jnp.float32)],
        compiler_params=room(12),
        cost_estimate=cost(2 * vocab * w.shape[1] * tokens, 8 * vocab * tokens),
        name="stats",
    )(normed, w, acc, ids)


def combine_kernel(x_ref, seq_ref, live_ref, logprob_ref, entropy_ref, sums_ref):
    top = x_ref[:, 0, :]
    total = x_ref[:, 1, :]
    best = jnp.max(top, axis=0, keepdims=True)
    gap = top - best
    scale = jnp.exp(gap)
    g_total = jnp.sum(total * scale, axis=0, keepdims=True)
    g_spread = jnp.sum((x_ref[:, 2, :] + gap * total) * scale, axis=0, keepdims=True)
    g_target = jnp.sum(x_ref[:, 3, :], axis=0, keepdims=True)
    live = live_ref[...]
    log_total = jnp.log(g_total)
    logprob = (g_target - best - log_total) * live
    entropy = (log_total - g_spread / g_total) * live
    tokens = top.shape[1]
    share = logprob_ref.shape[1]
    row = lax.broadcasted_iota(jnp.int32, (8, tokens), 0)
    rows = jnp.where(row == 0, logprob, jnp.where(row == 1, live, jnp.where(row == 2, entropy, 0.0)))
    seat = lax.broadcasted_iota(jnp.int32, (2 * SEQS, tokens), 0)
    member = (seat % SEQS == seq_ref[...]).astype(jnp.float32)
    token = lax.broadcasted_iota(jnp.int32, (2 * SEQS, tokens), 1)
    mine = (token == seat + lax.axis_index("tensor") * share).astype(jnp.float32)
    exact = functools.partial(
        lax.dot_general,
        dimension_numbers=NT,
        precision=lax.Precision.HIGHEST,
        preferred_element_type=jnp.float32,
    )
    sums, own = exact(rows, member), exact(rows, mine)
    lane = lax.broadcasted_iota(jnp.int32, (1, 2 * SEQS), 1)
    sums_ref[...] = jnp.where(lane < SEQS, sums[0:1, :], sums[1:2, :])
    logprob_ref[...] = own[0:1, 0:share]
    entropy_ref[...] = own[2:3, 0:share]


def combine(x, seq, live):
    row = jax.ShapeDtypeStruct((1, x.shape[2] // x.shape[0]), jnp.float32)
    return pl.pallas_call(
        combine_kernel,
        out_shape=(row, row, jax.ShapeDtypeStruct((1, 2 * SEQS), jnp.float32)),
        in_specs=[VM] * 3,
        out_specs=(VM, VM, VM),
        compiler_params=room(8),
        name="combine",
    )(x, seq, live)


def body(hidden, gain, head_weight, targets, seq_ids, live):
    shards = lax.axis_size("tensor")
    ring = lax.axis_size("dp")
    tokens = hidden.shape[0]
    share = tokens // shards

    forth = [(i, (i + 1) % ring) for i in range(ring)]
    back = [(i, (i - 1) % ring) for i in range(ring)]
    own = head_weight.T
    chunks = [own]

    def turn(a, b, s):
        a = lax.ppermute(a, "dp", forth)
        if s < ring - s:
            b = lax.ppermute(b, "dp", back)
            return a, b
        return a, None

    a, b = turn(own, own, 1)
    chunks += [a, b]
    teams = [[t for t in range(shards) if t % 2 == c] for c in range(2)]
    sent = fan(hidden, gain, seq_ids, live, shards // 2)
    one = lax.all_to_all(sent, "tensor", 0, 0, axis_index_groups=teams)
    two = lax.ppermute(one, "tensor", [(t, t ^ 1) for t in range(shards)])
    normed, extra = normalise(one, two)
    for s in range(2, ring // 2):
        a, b = turn(a, b, s)
        chunks += [a, b]
    last, _ = turn(a, b, ring // 2)
    aheads = [0] + [s if i else -s for s in range(1, ring // 2 + 1) for i in range(2)]
    acc = accumulate(aheads[0:9], normed, chunks[0:9])
    acc = accumulate(aheads[9:15], normed, chunks[9:15], acc)
    flags = extra[:, :, 1:3, :share].transpose(2, 1, 0, 3).reshape(2, 1, tokens)
    seq, alive = flags[0].astype(jnp.int32), flags[1]
    stats = statistics(ring // 2, normed, last, acc, targets)

    everyone = lax.all_to_all(
        jnp.broadcast_to(stats[None], (shards, *stats.shape)), "tensor", 0, 0
    )
    logprob, entropy, sums = combine(everyone, seq, alive)
    planes = lax.all_to_all(jnp.broadcast_to(sums, (ring, 2 * SEQS)), "dp", 0, 0)
    whole = jnp.sum(planes, axis=0)
    seq_mean = whole[:SEQS] / jnp.maximum(whole[SEQS:], 1.0)
    return logprob[0], entropy[0], seq_mean


def solution(mesh):
    placed = (
        P("dp", "tensor"),
        P("tensor"),
        P("dp", "tensor"),
        P("dp"),
        P(("dp", "tensor")),
        P(("dp", "tensor")),
    )

    return jax.shard_map(
        body,
        mesh=mesh,
        in_specs=placed,
        out_specs=(P(("dp", "tensor")), P(("dp", "tensor")), P()),
        check_vma=False,
    )
```

```python
import functools

import jax
import jax.numpy as jnp
from jax import lax
from jax.experimental import pallas as pl
from jax.experimental.pallas import tpu as pltpu
from jax.sharding import PartitionSpec as P


SEQS = 64
EXTRA = 16
VM = pl.BlockSpec(memory_space=pltpu.VMEM)
NT = (((1,), (1,)), ((), ()))


def room(mib):
    return pltpu.CompilerParams(vmem_limit_bytes=mib << 20)


def cost(flops, nbytes):
    return pl.CostEstimate(flops=int(flops), transcendentals=0, bytes_accessed=int(nbytes))


def fan_kernel(hid_ref, gain_ref, seq_ref, live_ref, out_ref, block_ref, g_ref, s_ref, l_ref, extra_ref, sems):
    copies, rows, _ = out_ref.shape
    share = seq_ref.shape[1]
    loads = [
        pltpu.make_async_copy(gain_ref, g_ref, sems.at[0]),
        pltpu.make_async_copy(seq_ref, s_ref, sems.at[1]),
        pltpu.make_async_copy(live_ref, l_ref, sems.at[2]),
        pltpu.make_async_copy(hid_ref, block_ref.at[pl.ds(0, rows - EXTRA)], sems.at[3]),
    ]
    for load in loads:
        load.start()
    for load in loads:
        load.wait()
    extra_ref[...] = jnp.zeros_like(extra_ref)
    extra_ref[0:1, :] = g_ref[...].astype(jnp.float32)
    extra_ref[1:2, 0:share] = s_ref[...].astype(jnp.float32)
    extra_ref[2:3, 0:share] = l_ref[...].astype(jnp.float32)
    block_ref[rows - EXTRA : rows, :] = extra_ref[...].astype(jnp.bfloat16)
    moves = [pltpu.make_async_copy(block_ref, out_ref.at[i], sems.at[i]) for i in range(copies)]
    for move in moves:
        move.start()
    for move in moves:
        move.wait()


def fan(hidden, gain, seq_ids, live, copies):
    tokens, lanes = hidden.shape
    share = seq_ids.shape[0]
    return pl.pallas_call(
        fan_kernel,
        out_shape=pltpu.HBM((copies, tokens + EXTRA, lanes), jnp.bfloat16),
        in_specs=[pl.BlockSpec(memory_space=pltpu.HBM)] * 4,
        out_specs=pl.BlockSpec(memory_space=pltpu.HBM),
        scratch_shapes=[
            pltpu.VMEM((tokens + EXTRA, lanes), jnp.bfloat16),
            pltpu.VMEM((1, lanes), jnp.bfloat16),
            pltpu.VMEM((1, share), jnp.int32),
            pltpu.VMEM((1, share), jnp.int32),
            pltpu.VMEM((EXTRA, lanes), jnp.float32),
            pltpu.SemaphoreType.DMA((copies,)),
        ],
        compiler_params=room(4),
        name="fan",
    )(*(pltpu.with_memory_space_constraint(x, pltpu.HBM) for x in (hidden, gain[None], seq_ids[None], live[None])))


def norm_kernel(one_ref, two_ref, gain_one_ref, gain_two_ref, out_ref, flag_ref):
    chips, step, lanes = one_ref.shape
    core = lax.axis_index("tensor") % 2

    @pl.when(pl.program_id(0) == 0)
    def _():
        flag_ref[core] = gain_one_ref[...].astype(jnp.float32)
        flag_ref[1 - core] = gain_two_ref[...].astype(jnp.float32)

    square = jnp.zeros((step, lanes), jnp.float32)
    for ref in (one_ref, two_ref):
        for t in range(chips):
            v = ref[t].astype(jnp.float32)
            square = square + v * v
    mean = jnp.sum(square, axis=-1, keepdims=True) / (2 * chips * lanes)
    scale = lax.rsqrt(mean + 1e-05)
    for ref, gain_ref, half in ((one_ref, gain_one_ref, core), (two_ref, gain_two_ref, 1 - core)):
        to = pl.ds(pl.multiple_of(half * lanes, lanes), lanes)
        for t in range(chips):
            gain = gain_ref[t].astype(jnp.float32)[0:1, :]
            out_ref[t, :, to] = (ref[t].astype(jnp.float32) * scale * gain).astype(jnp.bfloat16)


def normalise(one, two):
    chips, rows, lanes = one.shape
    tokens, step = rows - EXTRA, 128
    part = pl.BlockSpec((chips, step, lanes), lambda i: (0, i, 0))
    gain = pl.BlockSpec((chips, EXTRA, lanes), lambda i: (0, tokens // EXTRA, 0))
    return pl.pallas_call(
        norm_kernel,
        grid=(tokens // step,),
        out_shape=(
            jax.ShapeDtypeStruct((chips, tokens, 2 * lanes), jnp.bfloat16),
            jax.ShapeDtypeStruct((2, chips, EXTRA, lanes), jnp.float32),
        ),
        in_specs=[part, part, gain, gain],
        out_specs=(
            pl.BlockSpec((chips, step, 2 * lanes), lambda i: (0, i, 0)),
            pl.BlockSpec((2, chips, EXTRA, lanes), lambda i: (0, 0, 0, 0)),
        ),
        compiler_params=room(8),
        cost_estimate=cost(12 * one.size, 8 * one.size),
        name="norm",
    )(one, two, one, two)


def product(w, x):
    return lax.dot_general(w, x, NT, preferred_element_type=jnp.float32)


def blocks_of(tokens, width=256):
    return [slice(i, min(i + width, tokens)) for i in range(0, tokens, width)]


def row_block(ahead):
    return (lax.axis_index("dp") + ahead) % lax.axis_size("dp")


def mm_kernel(aheads, n_ref, *refs):
    count = len(aheads)
    ws, out_ref = refs[:count], refs[-1]
    fresh = len(refs) == count + 1
    at = [row_block(ahead + n_ref.shape[0]) for ahead in aheads]
    for cols in blocks_of(n_ref.shape[1]):
        total = None if fresh else refs[count][:, cols]
        for i in range(count):
            d = product(ws[i][...], n_ref[at[i], cols, :])
            total = d if total is None else total + d
        out_ref[:, cols] = total


def accumulate(aheads, normed, ws, acc=None):
    vocab, depth = ws[0].shape
    tokens = normed.shape[1]
    return pl.pallas_call(
        functools.partial(mm_kernel, tuple(aheads)),
        out_shape=jax.ShapeDtypeStruct((vocab, tokens), jnp.float32),
        in_specs=[VM] * (1 + len(ws)) + ([] if acc is None else [VM]),
        out_specs=VM,
        input_output_aliases={} if acc is None else {1 + len(ws): 0},
        compiler_params=room(12),
        cost_estimate=cost(2 * len(ws) * vocab * depth * tokens, 8 * vocab * tokens),
        name="scores",
    )(normed, *ws, *([] if acc is None else [acc]))


def stats_kernel(ahead, n_ref, w_ref, acc_ref, ids_ref, out_ref, s_ref):
    vocab, tokens = acc_ref.shape
    at = row_block(ahead)
    first = lax.axis_index("tensor") * vocab
    for cols in blocks_of(tokens):
        s_ref[:, cols] = acc_ref[:, cols] + product(w_ref[...], n_ref[at, cols, :])
    for j in range(tokens // 128):
        at = slice(j * 128, (j + 1) * 128)
        s = s_ref[:, at]
        top = jnp.max(s, axis=0, keepdims=True)
        row = lax.broadcasted_iota(jnp.int32, s.shape, 0)
        picked = jnp.sum(jnp.where(row == ids_ref[at][None] - first, s, 0.0), axis=0, keepdims=True)
        shifted = s - top
        expo = jnp.exp(shifted)
        total = jnp.sum(expo, axis=0, keepdims=True)
        spread = jnp.sum(expo * shifted, axis=0, keepdims=True)
        out_ref[0:1, at] = top
        out_ref[1:2, at] = total
        out_ref[2:3, at] = spread
        out_ref[3:4, at] = picked


def statistics(ahead, normed, w, acc, ids):
    vocab, tokens = acc.shape
    return pl.pallas_call(
        functools.partial(stats_kernel, ahead),
        out_shape=jax.ShapeDtypeStruct((4, tokens), jnp.float32),
        in_specs=[VM] * 4,
        out_specs=VM,
        scratch_shapes=[pltpu.VMEM((vocab, tokens), jnp.float32)],
        compiler_params=room(12),
        cost_estimate=cost(2 * vocab * w.shape[1] * tokens, 8 * vocab * tokens),
        name="stats",
    )(normed, w, acc, ids)


def combine_kernel(x_ref, seq_ref, live_ref, logprob_ref, entropy_ref, sums_ref):
    top = x_ref[:, 0, :]
    total = x_ref[:, 1, :]
    best = jnp.max(top, axis=0, keepdims=True)
    gap = top - best
    scale = jnp.exp(gap)
    g_total = jnp.sum(total * scale, axis=0, keepdims=True)
    g_spread = jnp.sum((x_ref[:, 2, :] + gap * total) * scale, axis=0, keepdims=True)
    g_target = jnp.sum(x_ref[:, 3, :], axis=0, keepdims=True)
    live = live_ref[...]
    log_total = jnp.log(g_total)
    logprob = (g_target - best - log_total) * live
    entropy = (log_total - g_spread / g_total) * live
    tokens = top.shape[1]
    share = logprob_ref.shape[1]
    row = lax.broadcasted_iota(jnp.int32, (8, tokens), 0)
    rows = jnp.where(row == 0, logprob, jnp.where(row == 1, live, jnp.where(row == 2, entropy, 0.0)))
    seat = lax.broadcasted_iota(jnp.int32, (2 * SEQS, tokens), 0)
    member = (seat % SEQS == seq_ref[...]).astype(jnp.float32)
    token = lax.broadcasted_iota(jnp.int32, (2 * SEQS, tokens), 1)
    mine = (token == seat + lax.axis_index("tensor") * share).astype(jnp.float32)
    exact = functools.partial(
        lax.dot_general,
        dimension_numbers=NT,
        precision=lax.Precision.HIGHEST,
        preferred_element_type=jnp.float32,
    )
    sums, own = exact(rows, member), exact(rows, mine)
    lane = lax.broadcasted_iota(jnp.int32, (1, 2 * SEQS), 1)
    sums_ref[...] = jnp.where(lane < SEQS, sums[0:1, :], sums[1:2, :])
    logprob_ref[...] = own[0:1, 0:share]
    entropy_ref[...] = own[2:3, 0:share]


def combine(x, seq, live):
    row = jax.ShapeDtypeStruct((1, x.shape[2] // x.shape[0]), jnp.float32)
    return pl.pallas_call(
        combine_kernel,
        out_shape=(row, row, jax.ShapeDtypeStruct((1, 2 * SEQS), jnp.float32)),
        in_specs=[VM] * 3,
        out_specs=(VM, VM, VM),
        compiler_params=room(8),
        name="combine",
    )(x, seq, live)


def body(hidden, gain, head_weight, targets, seq_ids, live):
    shards = lax.axis_size("tensor")
    ring = lax.axis_size("dp")
    tokens = hidden.shape[0]
    share = tokens // shards

    forth = [(i, (i + 1) % ring) for i in range(ring)]
    back = [(i, (i - 1) % ring) for i in range(ring)]
    own = head_weight.T
    chunks = [own]

    def turn(a, b, s):
        a = lax.ppermute(a, "dp", forth)
        if s < ring - s:
            b = lax.ppermute(b, "dp", back)
            return a, b
        return a, None

    a, b = turn(own, own, 1)
    chunks += [a, b]
    teams = [[t for t in range(shards) if t % 2 == c] for c in range(2)]
    sent = fan(hidden, gain, seq_ids, live, shards // 2)
    one = lax.all_to_all(sent, "tensor", 0, 0, axis_index_groups=teams)
    two = lax.ppermute(one, "tensor", [(t, t ^ 1) for t in range(shards)])
    normed, extra = normalise(one, two)
    for s in range(2, ring // 2):
        a, b = turn(a, b, s)
        chunks += [a, b]
    last, _ = turn(a, b, ring // 2)
    aheads = [0] + [s if i else -s for s in range(1, ring // 2 + 1) for i in range(2)]
    acc = accumulate(aheads[0:7], normed, chunks[0:7])
    acc = accumulate(aheads[7:15], normed, chunks[7:15], acc)
    flags = extra[:, :, 1:3, :share].transpose(2, 1, 0, 3).reshape(2, 1, tokens)
    seq, alive = flags[0].astype(jnp.int32), flags[1]
    stats = statistics(ring // 2, normed, last, acc, targets)

    everyone = lax.all_to_all(
        jnp.broadcast_to(stats[None], (shards, *stats.shape)), "tensor", 0, 0
    )
    logprob, entropy, sums = combine(everyone, seq, alive)
    planes = lax.all_to_all(jnp.broadcast_to(sums, (ring, 2 * SEQS)), "dp", 0, 0)
    whole = jnp.sum(planes, axis=0)
    seq_mean = whole[:SEQS] / jnp.maximum(whole[SEQS:], 1.0)
    return logprob[0], entropy[0], seq_mean


def solution(mesh):
    placed = (
        P("dp", "tensor"),
        P("tensor"),
        P("dp", "tensor"),
        P("dp"),
        P(("dp", "tensor")),
        P(("dp", "tensor")),
    )

    return jax.shard_map(
        body,
        mesh=mesh,
        in_specs=placed,
        out_specs=(P(("dp", "tensor")), P(("dp", "tensor")), P()),
        check_vma=False,
    )
```

```python
import functools

import jax
import jax.numpy as jnp
from jax import lax
from jax.experimental import pallas as pl
from jax.experimental.pallas import tpu as pltpu
from jax.sharding import PartitionSpec as P


SEQS = 64
EXTRA = 16
VM = pl.BlockSpec(memory_space=pltpu.VMEM)
NT = (((1,), (1,)), ((), ()))


def room(mib):
    return pltpu.CompilerParams(vmem_limit_bytes=mib << 20)


def cost(flops, nbytes):
    return pl.CostEstimate(flops=int(flops), transcendentals=0, bytes_accessed=int(nbytes))


def fan_kernel(hid_ref, gain_ref, seq_ref, live_ref, out_ref, block_ref, g_ref, s_ref, l_ref, extra_ref, sems):
    copies, rows, _ = out_ref.shape
    share = seq_ref.shape[1]
    loads = [
        pltpu.make_async_copy(gain_ref, g_ref, sems.at[0]),
        pltpu.make_async_copy(seq_ref, s_ref, sems.at[1]),
        pltpu.make_async_copy(live_ref, l_ref, sems.at[2]),
        pltpu.make_async_copy(hid_ref, block_ref.at[pl.ds(0, rows - EXTRA)], sems.at[3]),
    ]
    for load in loads:
        load.start()
    for load in loads:
        load.wait()
    extra_ref[...] = jnp.zeros_like(extra_ref)
    extra_ref[0:1, :] = g_ref[...].astype(jnp.float32)
    extra_ref[1:2, 0:share] = s_ref[...].astype(jnp.float32)
    extra_ref[2:3, 0:share] = l_ref[...].astype(jnp.float32)
    block_ref[rows - EXTRA : rows, :] = extra_ref[...].astype(jnp.bfloat16)
    moves = [pltpu.make_async_copy(block_ref, out_ref.at[i], sems.at[i]) for i in range(copies)]
    for move in moves:
        move.start()
    for move in moves:
        move.wait()


def fan(hidden, gain, seq_ids, live, copies):
    tokens, lanes = hidden.shape
    share = seq_ids.shape[0]
    return pl.pallas_call(
        fan_kernel,
        out_shape=pltpu.HBM((copies, tokens + EXTRA, lanes), jnp.bfloat16),
        in_specs=[pl.BlockSpec(memory_space=pltpu.HBM)] * 4,
        out_specs=pl.BlockSpec(memory_space=pltpu.HBM),
        scratch_shapes=[
            pltpu.VMEM((tokens + EXTRA, lanes), jnp.bfloat16),
            pltpu.VMEM((1, lanes), jnp.bfloat16),
            pltpu.VMEM((1, share), jnp.int32),
            pltpu.VMEM((1, share), jnp.int32),
            pltpu.VMEM((EXTRA, lanes), jnp.float32),
            pltpu.SemaphoreType.DMA((copies,)),
        ],
        compiler_params=room(4),
        name="fan",
    )(
        *(
            pltpu.with_memory_space_constraint(x, pltpu.HBM)
            for x in (hidden, gain[None], seq_ids[None], live[None])
        )
    )


def norm_kernel(one_ref, two_ref, out_ref, flag_ref, buf_ref, sems):
    _, chips, rows, lanes = buf_ref.shape
    tokens, step = rows - EXTRA, 128
    core = lax.axis_index("tensor") % 2

    def load(i, first, size):
        span = pl.ds(first, size)
        return [
            pltpu.make_async_copy(ref.at[:, span, :], buf_ref.at[r, :, span, :], sems.at[r, i])
            for r, ref in enumerate((one_ref, two_ref))
        ]

    count = tokens // step
    under = load(count, tokens, EXTRA)
    for copy in sum((load(i, i * step, step) for i in range(count)), under):
        copy.start()
    for copy in under:
        copy.wait()
    for r, half in enumerate((core, 1 - core)):
        flag_ref[half] = buf_ref[r, :, tokens:rows, :].astype(jnp.float32)

    def block(i, carry):
        first = pl.multiple_of(i * step, step)
        for copy in load(i, first, step):
            copy.wait()
        at = pl.ds(first, step)
        square = jnp.zeros((step, lanes), jnp.float32)
        for r in range(2):
            for t in range(chips):
                v = buf_ref[r, t, at, :].astype(jnp.float32)
                square = square + v * v
        mean = jnp.sum(square, axis=-1, keepdims=True) / (2 * chips * lanes)
        scale = lax.rsqrt(mean + 1e-05)
        for r, half in enumerate((core, 1 - core)):
            to = pl.ds(pl.multiple_of(half * lanes, lanes), lanes)
            for t in range(chips):
                v = buf_ref[r, t, at, :].astype(jnp.float32)
                gain = flag_ref[half, t, 0:1, :]
                out_ref[t, at, to] = (v * scale * gain).astype(jnp.bfloat16)
        return carry

    lax.fori_loop(0, count, block, 0)


def normalise(one, two):
    chips, rows, lanes = one.shape
    tokens = rows - EXTRA
    return pl.pallas_call(
        norm_kernel,
        out_shape=(
            jax.ShapeDtypeStruct((chips, tokens, 2 * lanes), jnp.bfloat16),
            jax.ShapeDtypeStruct((2, chips, EXTRA, lanes), jnp.float32),
        ),
        in_specs=[pl.BlockSpec(memory_space=pl.ANY)] * 2,
        out_specs=(VM, VM),
        scratch_shapes=[
            pltpu.VMEM((2, chips, rows, lanes), jnp.bfloat16),
            pltpu.SemaphoreType.DMA((2, tokens // 128 + 1)),
        ],
        compiler_params=room(12),
        cost_estimate=cost(12 * one.size, 8 * one.size),
        name="norm",
    )(one, two)


def product(w, x):
    return lax.dot_general(w, x, NT, preferred_element_type=jnp.float32)


def blocks_of(tokens, width=256):
    return [slice(i, min(i + width, tokens)) for i in range(0, tokens, width)]


def row_block(ahead):
    return (lax.axis_index("dp") + ahead) % lax.axis_size("dp")


def mm_kernel(aheads, n_ref, *refs):
    count = len(aheads)
    ws, out_ref = refs[:count], refs[-1]
    fresh = len(refs) == count + 1
    at = [row_block(ahead + n_ref.shape[0]) for ahead in aheads]
    for cols in blocks_of(n_ref.shape[1]):
        total = None if fresh else refs[count][:, cols]
        for i in range(count):
            d = product(ws[i][...], n_ref[at[i], cols, :])
            total = d if total is None else total + d
        out_ref[:, cols] = total


def accumulate(aheads, normed, ws, acc=None):
    vocab, depth = ws[0].shape
    tokens = normed.shape[1]
    return pl.pallas_call(
        functools.partial(mm_kernel, tuple(aheads)),
        out_shape=jax.ShapeDtypeStruct((vocab, tokens), jnp.float32),
        in_specs=[VM] * (1 + len(ws)) + ([] if acc is None else [VM]),
        out_specs=VM,
        input_output_aliases={} if acc is None else {1 + len(ws): 0},
        compiler_params=room(12),
        cost_estimate=cost(2 * len(ws) * vocab * depth * tokens, 8 * vocab * tokens),
        name="scores",
    )(normed, *ws, *([] if acc is None else [acc]))


def stats_kernel(ahead, n_ref, w_ref, acc_ref, ids_ref, out_ref, s_ref):
    vocab, tokens = acc_ref.shape
    at = row_block(ahead)
    first = lax.axis_index("tensor") * vocab
    for cols in blocks_of(tokens):
        s_ref[:, cols] = acc_ref[:, cols] + product(w_ref[...], n_ref[at, cols, :])
    for j in range(tokens // 128):
        at = slice(j * 128, (j + 1) * 128)
        s = s_ref[:, at]
        top = jnp.max(s, axis=0, keepdims=True)
        row = lax.broadcasted_iota(jnp.int32, s.shape, 0)
        picked = jnp.sum(jnp.where(row == ids_ref[at][None] - first, s, 0.0), axis=0, keepdims=True)
        shifted = s - top
        expo = jnp.exp(shifted)
        total = jnp.sum(expo, axis=0, keepdims=True)
        spread = jnp.sum(expo * shifted, axis=0, keepdims=True)
        out_ref[0:1, at] = top
        out_ref[1:2, at] = total
        out_ref[2:3, at] = spread
        out_ref[3:4, at] = picked


def statistics(ahead, normed, w, acc, ids):
    vocab, tokens = acc.shape
    return pl.pallas_call(
        functools.partial(stats_kernel, ahead),
        out_shape=jax.ShapeDtypeStruct((4, tokens), jnp.float32),
        in_specs=[VM] * 4,
        out_specs=VM,
        scratch_shapes=[pltpu.VMEM((vocab, tokens), jnp.float32)],
        compiler_params=room(12),
        cost_estimate=cost(2 * vocab * w.shape[1] * tokens, 8 * vocab * tokens),
        name="stats",
    )(normed, w, acc, ids)


def combine_kernel(x_ref, seq_ref, live_ref, logprob_ref, entropy_ref, sums_ref):
    top = x_ref[:, 0, :]
    total = x_ref[:, 1, :]
    best = jnp.max(top, axis=0, keepdims=True)
    gap = top - best
    scale = jnp.exp(gap)
    g_total = jnp.sum(total * scale, axis=0, keepdims=True)
    g_spread = jnp.sum((x_ref[:, 2, :] + gap * total) * scale, axis=0, keepdims=True)
    g_target = jnp.sum(x_ref[:, 3, :], axis=0, keepdims=True)
    live = live_ref[...]
    log_total = jnp.log(g_total)
    logprob = (g_target - best - log_total) * live
    entropy = (log_total - g_spread / g_total) * live
    tokens = top.shape[1]
    share = logprob_ref.shape[1]
    row = lax.broadcasted_iota(jnp.int32, (8, tokens), 0)
    rows = jnp.where(row == 0, logprob, jnp.where(row == 1, live, jnp.where(row == 2, entropy, 0.0)))
    seat = lax.broadcasted_iota(jnp.int32, (2 * SEQS, tokens), 0)
    member = (seat % SEQS == seq_ref[...]).astype(jnp.float32)
    token = lax.broadcasted_iota(jnp.int32, (2 * SEQS, tokens), 1)
    mine = (token == seat + lax.axis_index("tensor") * share).astype(jnp.float32)
    exact = functools.partial(
        lax.dot_general,
        dimension_numbers=NT,
        precision=lax.Precision.HIGHEST,
        preferred_element_type=jnp.float32,
    )
    sums, own = exact(rows, member), exact(rows, mine)
    lane = lax.broadcasted_iota(jnp.int32, (1, 2 * SEQS), 1)
    sums_ref[...] = jnp.where(lane < SEQS, sums[0:1, :], sums[1:2, :])
    logprob_ref[...] = own[0:1, 0:share]
    entropy_ref[...] = own[2:3, 0:share]


def combine(x, seq, live):
    row = jax.ShapeDtypeStruct((1, x.shape[2] // x.shape[0]), jnp.float32)
    return pl.pallas_call(
        combine_kernel,
        out_shape=(row, row, jax.ShapeDtypeStruct((1, 2 * SEQS), jnp.float32)),
        in_specs=[VM] * 3,
        out_specs=(VM, VM, VM),
        compiler_params=room(8),
        name="combine",
    )(x, seq, live)


def body(hidden, gain, head_weight, targets, seq_ids, live):
    shards = lax.axis_size("tensor")
    ring = lax.axis_size("dp")
    tokens = hidden.shape[0]
    share = tokens // shards

    forth = [(i, (i + 1) % ring) for i in range(ring)]
    back = [(i, (i - 1) % ring) for i in range(ring)]
    own = head_weight.T
    chunks = [own]

    def turn(a, b, s):
        a = lax.ppermute(a, "dp", forth)
        if s < ring - s:
            b = lax.ppermute(b, "dp", back)
            return a, b
        return a, None

    a, b = turn(own, own, 1)
    chunks += [a, b]
    teams = [[t for t in range(shards) if t % 2 == c] for c in range(2)]
    sent = fan(hidden, gain, seq_ids, live, shards // 2)
    one = lax.all_to_all(sent, "tensor", 0, 0, axis_index_groups=teams)
    two = lax.ppermute(one, "tensor", [(t, t ^ 1) for t in range(shards)])
    normed, extra = normalise(one, two)
    for s in range(2, ring // 2):
        a, b = turn(a, b, s)
        chunks += [a, b]
    last, _ = turn(a, b, ring // 2)
    aheads = [0] + [s if i else -s for s in range(1, ring // 2 + 1) for i in range(2)]
    acc = accumulate(aheads[0:5], normed, chunks[0:5])
    acc = accumulate(aheads[5:15], normed, chunks[5:15], acc)
    flags = extra[:, :, 1:3, :share].transpose(2, 1, 0, 3).reshape(2, 1, tokens)
    seq, alive = flags[0].astype(jnp.int32), flags[1]
    stats = statistics(ring // 2, normed, last, acc, targets)

    everyone = lax.all_to_all(
        jnp.broadcast_to(stats[None], (shards, *stats.shape)), "tensor", 0, 0
    )
    logprob, entropy, sums = combine(everyone, seq, alive)
    planes = lax.all_to_all(jnp.broadcast_to(sums, (ring, 2 * SEQS)), "dp", 0, 0)
    whole = jnp.sum(planes, axis=0)
    seq_mean = whole[:SEQS] / jnp.maximum(whole[SEQS:], 1.0)
    return logprob[0], entropy[0], seq_mean


def solution(mesh):
    placed = (
        P("dp", "tensor"),
        P("tensor"),
        P("dp", "tensor"),
        P("dp"),
        P(("dp", "tensor")),
        P(("dp", "tensor")),
    )

    return jax.shard_map(
        body,
        mesh=mesh,
        in_specs=placed,
        out_specs=(P(("dp", "tensor")), P(("dp", "tensor")), P()),
        check_vma=False,
    )
```

```python
import functools

import jax
import jax.numpy as jnp
from jax import lax
from jax.experimental import pallas as pl
from jax.experimental.pallas import tpu as pltpu
from jax.sharding import PartitionSpec as P


SEQS = 64
EXTRA = 16
VM = pl.BlockSpec(memory_space=pltpu.VMEM)
NT = (((1,), (1,)), ((), ()))


def room(mib):
    return pltpu.CompilerParams(vmem_limit_bytes=mib << 20)


def cost(flops, nbytes):
    return pl.CostEstimate(flops=int(flops), transcendentals=0, bytes_accessed=int(nbytes))


def fan_kernel(hid_ref, gain_ref, seq_ref, live_ref, out_ref, block_ref, g_ref, s_ref, l_ref, extra_ref, sems):
    copies, rows, _ = out_ref.shape
    share = seq_ref.shape[1]
    loads = [
        pltpu.make_async_copy(gain_ref, g_ref, sems.at[0]),
        pltpu.make_async_copy(seq_ref, s_ref, sems.at[1]),
        pltpu.make_async_copy(live_ref, l_ref, sems.at[2]),
        pltpu.make_async_copy(hid_ref, block_ref.at[pl.ds(0, rows - EXTRA)], sems.at[3]),
    ]
    for load in loads:
        load.start()
    for load in loads:
        load.wait()
    extra_ref[...] = jnp.zeros_like(extra_ref)
    extra_ref[0:1, :] = g_ref[...].astype(jnp.float32)
    extra_ref[1:2, 0:share] = s_ref[...].astype(jnp.float32)
    extra_ref[2:3, 0:share] = l_ref[...].astype(jnp.float32)
    block_ref[rows - EXTRA : rows, :] = extra_ref[...].astype(jnp.bfloat16)
    moves = [pltpu.make_async_copy(block_ref, out_ref.at[i], sems.at[i]) for i in range(copies)]
    for move in moves:
        move.start()
    for move in moves:
        move.wait()


def fan(hidden, gain, seq_ids, live, copies):
    tokens, lanes = hidden.shape
    share = seq_ids.shape[0]
    return pl.pallas_call(
        fan_kernel,
        out_shape=pltpu.HBM((copies, tokens + EXTRA, lanes), jnp.bfloat16),
        in_specs=[pl.BlockSpec(memory_space=pltpu.HBM)] * 4,
        out_specs=pl.BlockSpec(memory_space=pltpu.HBM),
        scratch_shapes=[
            pltpu.VMEM((tokens + EXTRA, lanes), jnp.bfloat16),
            pltpu.VMEM((1, lanes), jnp.bfloat16),
            pltpu.VMEM((1, share), jnp.int32),
            pltpu.VMEM((1, share), jnp.int32),
            pltpu.VMEM((EXTRA, lanes), jnp.float32),
            pltpu.SemaphoreType.DMA((copies,)),
        ],
        compiler_params=room(4),
        name="fan",
    )(
        *(
            pltpu.with_memory_space_constraint(x, pltpu.HBM)
            for x in (hidden, gain[None], seq_ids[None], live[None])
        )
    )


def norm_kernel(one_ref, two_ref, out_ref, flag_ref, buf_ref, sems):
    _, chips, rows, lanes = buf_ref.shape
    tokens, step = rows - EXTRA, 128
    core = lax.axis_index("tensor") % 2

    def load(i, first, size):
        span = pl.ds(first, size)
        return [
            pltpu.make_async_copy(ref.at[:, span, :], buf_ref.at[r, :, span, :], sems.at[r, i])
            for r, ref in enumerate((one_ref, two_ref))
        ]

    count = tokens // step
    under = load(count, tokens, EXTRA)
    for copy in sum((load(i, i * step, step) for i in range(count)), under):
        copy.start()
    for copy in under:
        copy.wait()
    for r, half in enumerate((core, 1 - core)):
        flag_ref[half] = buf_ref[r, :, tokens:rows, :].astype(jnp.float32)

    def block(i, carry):
        first = pl.multiple_of(i * step, step)
        for copy in load(i, first, step):
            copy.wait()
        at = pl.ds(first, step)
        square = jnp.zeros((step, lanes), jnp.float32)
        for r in range(2):
            for t in range(chips):
                v = buf_ref[r, t, at, :].astype(jnp.float32)
                square = square + v * v
        mean = jnp.sum(square, axis=-1, keepdims=True) / (2 * chips * lanes)
        scale = lax.rsqrt(mean + 1e-05)
        for r, half in enumerate((core, 1 - core)):
            to = pl.ds(pl.multiple_of(half * lanes, lanes), lanes)
            for t in range(chips):
                v = buf_ref[r, t, at, :].astype(jnp.float32)
                gain = flag_ref[half, t, 0:1, :]
                out_ref[t, at, to] = (v * scale * gain).astype(jnp.bfloat16)
        return carry

    lax.fori_loop(0, count, block, 0)


def normalise(one, two):
    chips, rows, lanes = one.shape
    tokens = rows - EXTRA
    return pl.pallas_call(
        norm_kernel,
        out_shape=(
            jax.ShapeDtypeStruct((chips, tokens, 2 * lanes), jnp.bfloat16),
            jax.ShapeDtypeStruct((2, chips, EXTRA, lanes), jnp.float32),
        ),
        in_specs=[pl.BlockSpec(memory_space=pl.ANY)] * 2,
        out_specs=(VM, VM),
        scratch_shapes=[
            pltpu.VMEM((2, chips, rows, lanes), jnp.bfloat16),
            pltpu.SemaphoreType.DMA((2, tokens // 128 + 1)),
        ],
        compiler_params=room(12),
        cost_estimate=cost(12 * one.size, 8 * one.size),
        name="norm",
    )(one, two)


def product(w, x):
    return lax.dot_general(w, x, NT, preferred_element_type=jnp.float32)


def blocks_of(tokens, width=256):
    return [slice(i, min(i + width, tokens)) for i in range(0, tokens, width)]


def row_block(ahead):
    return (lax.axis_index("dp") + ahead) % lax.axis_size("dp")


def mm_kernel(aheads, n_ref, *refs):
    count = len(aheads)
    ws, out_ref = refs[:count], refs[-1]
    fresh = len(refs) == count + 1
    at = [row_block(ahead + n_ref.shape[0]) for ahead in aheads]
    for cols in blocks_of(n_ref.shape[1]):
        total = None if fresh else refs[count][:, cols]
        for i in range(count):
            d = product(ws[i][...], n_ref[at[i], cols, :])
            total = d if total is None else total + d
        out_ref[:, cols] = total


def accumulate(aheads, normed, ws, acc=None):
    vocab, depth = ws[0].shape
    tokens = normed.shape[1]
    return pl.pallas_call(
        functools.partial(mm_kernel, tuple(aheads)),
        out_shape=jax.ShapeDtypeStruct((vocab, tokens), jnp.float32),
        in_specs=[VM] * (1 + len(ws)) + ([] if acc is None else [VM]),
        out_specs=VM,
        input_output_aliases={} if acc is None else {1 + len(ws): 0},
        compiler_params=room(12),
        cost_estimate=cost(2 * len(ws) * vocab * depth * tokens, 8 * vocab * tokens),
        name="scores",
    )(normed, *ws, *([] if acc is None else [acc]))


def stats_kernel(ahead, n_ref, w_ref, acc_ref, ids_ref, copies_ref, s_ref, out_ref, sems):
    vocab, tokens = acc_ref.shape
    at = row_block(ahead)
    first = lax.axis_index("tensor") * vocab
    for cols in blocks_of(tokens):
        s_ref[:, cols] = acc_ref[:, cols] + product(w_ref[...], n_ref[at, cols, :])
    for j in range(tokens // 128):
        at = slice(j * 128, (j + 1) * 128)
        s = s_ref[:, at]
        top = jnp.max(s, axis=0, keepdims=True)
        row = lax.broadcasted_iota(jnp.int32, s.shape, 0)
        picked = jnp.sum(jnp.where(row == ids_ref[at][None] - first, s, 0.0), axis=0, keepdims=True)
        shifted = s - top
        expo = jnp.exp(shifted)
        total = jnp.sum(expo, axis=0, keepdims=True)
        spread = jnp.sum(expo * shifted, axis=0, keepdims=True)
        out_ref[0:1, at] = top
        out_ref[1:2, at] = total
        out_ref[2:3, at] = spread
        out_ref[3:4, at] = picked
    moves = [
        pltpu.make_async_copy(out_ref, copies_ref.at[i], sems.at[i])
        for i in range(copies_ref.shape[0])
    ]
    for move in moves:
        move.start()
    for move in moves:
        move.wait()


def statistics(ahead, normed, w, acc, ids, copies):
    vocab, tokens = acc.shape
    return pl.pallas_call(
        functools.partial(stats_kernel, ahead),
        out_shape=pltpu.HBM((copies, 4, tokens), jnp.float32),
        in_specs=[VM] * 4,
        out_specs=pl.BlockSpec(memory_space=pltpu.HBM),
        scratch_shapes=[
            pltpu.VMEM((vocab, tokens), jnp.float32),
            pltpu.VMEM((4, tokens), jnp.float32),
            pltpu.SemaphoreType.DMA((copies,)),
        ],
        compiler_params=room(12),
        cost_estimate=cost(2 * vocab * w.shape[1] * tokens, 8 * vocab * tokens),
        name="stats",
    )(normed, w, acc, ids)


exact = functools.partial(
    lax.dot_general,
    dimension_numbers=NT,
    precision=lax.Precision.HIGHEST,
    preferred_element_type=jnp.float32,
)


def combine_kernel(x_ref, seq_ref, live_ref, logprob_ref, entropy_ref, sums_ref):
    top = x_ref[:, 0, :]
    total = x_ref[:, 1, :]
    best = jnp.max(top, axis=0, keepdims=True)
    gap = top - best
    scale = jnp.exp(gap)
    g_total = jnp.sum(total * scale, axis=0, keepdims=True)
    g_spread = jnp.sum((x_ref[:, 2, :] + gap * total) * scale, axis=0, keepdims=True)
    g_target = jnp.sum(x_ref[:, 3, :], axis=0, keepdims=True)
    live = live_ref[...]
    log_total = jnp.log(g_total)
    logprob = (g_target - best - log_total) * live
    logprob_ref[...] = logprob
    entropy_ref[...] = (log_total - g_spread / g_total) * live
    tokens = top.shape[1]
    row = lax.broadcasted_iota(jnp.int32, (8, tokens), 0)
    rows = jnp.where(row == 0, logprob, jnp.where(row == 1, live, 0.0))
    seat = lax.broadcasted_iota(jnp.int32, (2 * SEQS, tokens), 0)
    sums = exact(rows, (seat % SEQS == seq_ref[...]).astype(jnp.float32))
    lane = lax.broadcasted_iota(jnp.int32, (1, 2 * SEQS), 1)
    sums_ref[...] = jnp.where(lane < SEQS, sums[0:1, :], sums[1:2, :])


def combine(x, seq, live):
    row = jax.ShapeDtypeStruct((1, x.shape[2]), jnp.float32)
    return pl.pallas_call(
        combine_kernel,
        out_shape=(row, row, jax.ShapeDtypeStruct((1, 2 * SEQS), jnp.float32)),
        in_specs=[VM] * 3,
        out_specs=(VM, VM, VM),
        compiler_params=room(8),
        name="combine",
    )(x, seq, live)


def pick_kernel(logprob_ref, entropy_ref, own_logprob_ref, own_entropy_ref):
    tokens, share = logprob_ref.shape[1], own_logprob_ref.shape[1]
    row = lax.broadcasted_iota(jnp.int32, (8, tokens), 0)
    rows = jnp.where(row == 0, logprob_ref[...], jnp.where(row == 1, entropy_ref[...], 0.0))
    seat = lax.broadcasted_iota(jnp.int32, (128, tokens), 0)
    token = lax.broadcasted_iota(jnp.int32, (128, tokens), 1)
    own = exact(rows, (token == seat + lax.axis_index("tensor") * share).astype(jnp.float32))
    own_logprob_ref[...] = own[0:1, 0:share]
    own_entropy_ref[...] = own[1:2, 0:share]


def pick(logprob, entropy, share):
    own = jax.ShapeDtypeStruct((1, share), jnp.float32)
    return pl.pallas_call(
        pick_kernel,
        out_shape=(own, own),
        in_specs=[VM] * 2,
        out_specs=(VM, VM),
        compiler_params=room(8),
        name="pick",
    )(logprob, entropy)


def body(hidden, gain, head_weight, targets, seq_ids, live):
    shards = lax.axis_size("tensor")
    ring = lax.axis_size("dp")
    tokens = hidden.shape[0]
    share = tokens // shards

    forth = [(i, (i + 1) % ring) for i in range(ring)]
    back = [(i, (i - 1) % ring) for i in range(ring)]
    own = head_weight.T
    chunks = [own]

    def turn(a, b, s):
        a = lax.ppermute(a, "dp", forth)
        if s < ring - s:
            b = lax.ppermute(b, "dp", back)
            return a, b
        return a, None

    a, b = turn(own, own, 1)
    chunks += [a, b]
    teams = [[t for t in range(shards) if t % 2 == c] for c in range(2)]
    sent = fan(hidden, gain, seq_ids, live, shards // 2)
    one = lax.all_to_all(sent, "tensor", 0, 0, axis_index_groups=teams)
    two = lax.ppermute(one, "tensor", [(t, t ^ 1) for t in range(shards)])
    normed, extra = normalise(one, two)
    for s in range(2, ring // 2):
        a, b = turn(a, b, s)
        chunks += [a, b]
    last, _ = turn(a, b, ring // 2)
    aheads = [0] + [s if i else -s for s in range(1, ring // 2 + 1) for i in range(2)]
    acc = accumulate(aheads[0:5], normed, chunks[0:5])
    acc = accumulate(aheads[5:15], normed, chunks[5:15], acc)
    flags = extra[:, :, 1:3, :share].transpose(2, 1, 0, 3).reshape(2, 1, tokens)
    seq, alive = flags[0].astype(jnp.int32), flags[1]
    stats = statistics(ring // 2, normed, last, acc, targets, shards)

    everyone = lax.all_to_all(stats, "tensor", 0, 0)
    logprob, entropy, sums = combine(everyone, seq, alive)
    planes = lax.all_to_all(jnp.broadcast_to(sums, (ring, 2 * SEQS)), "dp", 0, 0)
    whole = jnp.sum(planes, axis=0)
    seq_mean = whole[:SEQS] / jnp.maximum(whole[SEQS:], 1.0)
    own_logprob, own_entropy = pick(logprob, entropy, share)
    return own_logprob[0], own_entropy[0], seq_mean


def solution(mesh):
    placed = (
        P("dp", "tensor"),
        P("tensor"),
        P("dp", "tensor"),
        P("dp"),
        P(("dp", "tensor")),
        P(("dp", "tensor")),
    )

    return jax.shard_map(
        body,
        mesh=mesh,
        in_specs=placed,
        out_specs=(P(("dp", "tensor")), P(("dp", "tensor")), P()),
        check_vma=False,
    )
```
